32 devices in a mesh: rep: 8 (over y, x, core), shard: 4 (over z).
Axes of the slice: x: 2, y: 2, z: 4, core: 2. Of those that a mesh axis runs over, the one named last changes fastest.
Arguments:
- tokens: bfloat16 [8, 1024, 768], P('rep', 'shard'), may hold values from -6 to 6
- w_qkv: bfloat16 [3, 4, 192, 192], P(None, None, 'shard'), may hold values from -0.4375 to 0.4375
- b_qv: bfloat16 [2, 768], P(None, 'shard'), may hold values from -1.5 to 1.5
- w_attn: bfloat16 [768, 768], P('shard'), may hold values from -1.25 to 1.25
- b_attn: bfloat16 [768], P('shard'), may hold values from -1.5 to 1.5
- ln1_gain: bfloat16 [768], P('shard'), may hold values from 0.5 to 1.5
- ln1_bias: bfloat16 [768], P('shard'), may hold values from -1.5 to 1.5
- w_inter: bfloat16 [4, 192, 768], P(None, 'shard'), may hold values from -0.4375 to 0.4375
- b_inter: bfloat16 [3072], P('shard'), may hold values from -2.5 to 2.5
- w_output: bfloat16 [4, 768, 192], P(None, 'shard'), may hold values from -0.21875 to 0.21875
- b_output: bfloat16 [768], P('shard'), may hold values from -1.5 to 1.5
- ln2_gain: bfloat16 [768], P('shard'), may hold values from 0.5 to 1.5
- ln2_bias: bfloat16 [768], P('shard'), may hold values from -1.5 to 1.5
- segment_ids: int32 [8, 1024], P('rep'), may hold values from 0 to 6, as said below
- keep_mask: int32 [8, 1024], P('rep'), may hold values 0 or 1
- cotangent: bfloat16 [8, 1024, 768], P('rep', 'shard'), may hold values from -6 to 6
Outputs:
- output: bfloat16 [8, 1024, 768], P('rep', 'shard')
- d_tokens: float32 [8, 1024, 768], P('rep', 'shard')
- g_w_qkv: float32 [3, 4, 192, 192], P(None, None, 'shard')
- g_b_qv: float32 [2, 768], P(None, 'shard')
- g_w_attn: float32 [768, 768], P('shard')
- g_b_attn: float32 [768], P('shard')
- g_ln1_gain: float32 [768], P('shard')
- g_ln1_bias: float32 [768], P('shard')
- g_w_inter: float32 [4, 192, 768], P(None, 'shard')
- g_b_inter: float32 [3072], P('shard')
- g_w_output: float32 [4, 768, 192], P(None, 'shard')
- g_b_output: float32 [768], P('shard')
- g_ln2_gain: float32 [768], P('shard')
- g_ln2_bias: float32 [768], P('shard')
The draws below stay inside these ranges and needn't reach their ends.
Inputs may be any that keep to these rules, and one draw needn't show every extreme that they name: `segment_ids`: along each sequence the document numbers never fall and each number covers at least one position.
All inputs are finite; a program needn't handle non-finite values. No bound on the sum of `keep_mask` on one device may be relied on, other than what follows from the above.
Results may differ from the reference program's by a relative error of at most 0.012.
Values may be sent and summed in bfloat16 or wider, within the bound.
No kernel may reach another device: no remote copies, remote signals or barrier semaphores. Data moves between devices by JAX's collectives and lax.ppermute only.
A program may use at most 128 MiB of HBM per device.

```python
from functools import partial
import jax
import jax.numpy as jnp
from jax import lax

D = 768
HEADS = 12
HEAD = 64
FF = 3072
GROUPS = 4
TOK_SEQ = 256
SIDE_DOCS = 3
DG = 192
FG = 768
LEN = 1024
SEQS = 8


def side_cuts(key, span):
    places = jnp.arange(TOK_SEQ, dtype=jnp.int32)
    raw_score = jax.random.randint(key, (TOK_SEQ,), 0, TOK_SEQ, dtype=jnp.int32) * TOK_SEQ + places
    usable = (places >= 1) & (places < span)
    score = jnp.where(usable, raw_score, -1)
    above = usable[None, :] & (score[None, :] > score[:, None])
    rank = jnp.sum(above.astype(jnp.int32), axis=1)
    return (usable & (rank < SIDE_DOCS - 1)).astype(jnp.int32)


def one_row(key):
    key_head, key_tail, key_hcut, key_tcut = jax.random.split(key, 4)
    head_len = jax.random.randint(key_head, (), SIDE_DOCS, TOK_SEQ, dtype=jnp.int32)
    tail_len = jax.random.randint(key_tail, (), SIDE_DOCS, TOK_SEQ, dtype=jnp.int32)
    places = jnp.arange(TOK_SEQ, dtype=jnp.int32)
    head_flags = side_cuts(key_hcut, head_len) + (places == head_len).astype(jnp.int32)
    tail_cut = side_cuts(key_tcut, tail_len)
    shifted = places - (TOK_SEQ - tail_len)
    picked = jnp.take(tail_cut, jnp.clip(shifted, 0, TOK_SEQ - 1))
    tail_flags = ((shifted == 0) | (shifted >= 1) & (picked == 1)).astype(jnp.int32)
    middle = jnp.zeros((LEN - 2 * TOK_SEQ,), jnp.int32)
    flags = jnp.concatenate([head_flags, middle, tail_flags])
    return jnp.cumsum(flags).astype(jnp.int32)


def draw_segment_ids(key, part):
    row_keys = jax.random.split(jax.random.fold_in(key, 17), SEQS)
    return jax.vmap(one_row)(row_keys)


def place_ends(entries, rng, least, top_value):
    dims = entries.shape
    index_at = [jax.random.randint(jax.random.fold_in(rng, axis), (), 0, dims[axis]) for axis in range(len(dims))]
    entries = entries.at[tuple(index_at)].set(least)
    longest = dims.index(max(dims))
    index_at[longest] = (index_at[longest] + 1) % dims[longest]
    return entries.at[tuple(index_at)].set(top_value)


def levels(rng, dims, shards, smallest, largest):
    def one(position, shards_of):
        heights = jax.random.uniform(jax.random.fold_in(jax.random.fold_in(rng, 6), position), (shards_of,), jnp.float32, smallest / len(shards), largest / len(shards))
        return jnp.repeat(jnp.exp(heights), dims[position] // shards_of).reshape((-1,) + (1,) * (len(dims) - position - 1))

    gain = one(*shards[0])
    for cut in shards[1:]:
        gain = gain * one(*cut)
    return gain


def normal_values(rng, dims, deviation, bound, shards=(), kind=jnp.bfloat16):
    values = jax.random.normal(rng, dims, jnp.float32) * deviation
    if len(shards) > 0:
        values = levels(rng, dims, shards, -0.22, 0.18) * values
    return jnp.clip(values, min=-bound, max=bound).astype(kind)


def setup_inputs(seed: int = 0) -> dict:
    seeds = jax.random.split(jax.random.key(seed), 17)
    return {
        "tokens": normal_values(seeds[0], (SEQS, LEN, D), 1.0, 6.0, ((0, 8), (1, 4))),
        "w_qkv": normal_values(seeds[1], (3, GROUPS, DG, DG), DG ** -0.5, 0.4375, ((2, 4),)),
        "b_qv": normal_values(seeds[2], (2, D), 0.3, 1.5, ((1, 4),)),
        "w_attn": normal_values(seeds[3], (D, D), (D // 32) ** -0.5, 1.25, ((0, 4),)),
        "b_attn": normal_values(seeds[4], (D,), 0.3, 1.5, ((0, 4),)),
        "ln1_gain": jnp.clip(1.0 + 0.1 * jax.random.normal(seeds[5], (D,), jnp.float32), 0.5, 1.5).astype(jnp.bfloat16),
        "ln1_bias": normal_values(seeds[6], (D,), 0.3, 1.5, ((0, 4),)),
        "w_inter": normal_values(seeds[7], (GROUPS, DG, FG), DG ** -0.5, 0.4375, ((1, 4),)),
        "b_inter": normal_values(seeds[8], (FF,), 0.5, 2.5, ((0, 4),)),
        "w_output": normal_values(seeds[9], (GROUPS, FG, DG), FG ** -0.5, 0.21875, ((1, 4),)),
        "b_output": normal_values(seeds[10], (D,), 0.3, 1.5, ((0, 4),)),
        "ln2_gain": jnp.clip(1.0 + 0.1 * jax.random.normal(seeds[11], (D,), jnp.float32), 0.5, 1.5).astype(jnp.bfloat16),
        "ln2_bias": normal_values(seeds[12], (D,), 0.3, 1.5, ((0, 4),)),
        "segment_ids": draw_segment_ids(jax.random.fold_in(seeds[16], 71), 0),
        "keep_mask": place_ends((jax.random.randint(seeds[14], (SEQS, LEN), 0, 8) < 7).astype(jnp.int32), jax.random.fold_in(seeds[14], 1), 0, 1),
        "cotangent": normal_values(seeds[15], (SEQS, LEN, D), 1.0, 6.0, ((0, 8), (1, 4))),
    }


@jax.custom_vjp
def low(v):
    return lax.optimization_barrier(v.astype(jnp.bfloat16)).astype(jnp.float32)

@jax.custom_vjp
def low_back(v):
    return v

def low_keep(v):
    return (low(v), None)

def low_pass(kept, grad):
    return (grad,)

def back_keep(v):
    return (v, None)

def back_low(kept, grad):
    return (low(grad),)
low.defvjp(low_keep, low_pass)
low_back.defvjp(back_keep, back_low)
epsilon = 1e-05
masked_score = -1e+30
highest = lax.Precision.HIGHEST

def layer_norm(residual, gain_vec, shift_vec):
    centre = residual - lax.optimization_barrier(jnp.mean(residual, axis=-1, keepdims=True))
    spread = lax.optimization_barrier(jnp.mean(centre * centre, axis=-1, keepdims=True))
    return centre * lax.rsqrt(spread + epsilon) * gain_vec + shift_vec

def attend_head(operands, allowed):
    queries, keys, values = operands
    scores = low_back(jnp.einsum('qd,kd->qk', queries, keys, precision=highest) * HEAD ** (-0.5))
    masked = jnp.where(allowed, scores, masked_score)
    row_peak = lax.optimization_barrier(jnp.max(masked, axis=-1, keepdims=True))
    logsum = row_peak + jnp.log(lax.optimization_barrier(jnp.sum(jnp.exp(masked - row_peak), axis=-1, keepdims=True)))
    prob_low = low(jnp.exp(masked - logsum))
    return jnp.einsum('qk,kd->qd', prob_low, values, precision=highest)

def block_forward(tokens_f, w_qkv, b_qv, w_attn, b_attn, ln1_gain, ln1_bias, w_inter, b_inter, w_output, b_output, ln2_gain, ln2_bias, segments, keep_row):
    length = tokens_f.shape[0]
    grouped = tokens_f.reshape(length, GROUPS, D // GROUPS)
    qkv_mixed = jnp.einsum('lgc,kgcd->klgd', grouped, w_qkv, precision=highest).reshape(3, length, D)
    queries = low_back(low(qkv_mixed[0] + b_qv[0]))
    keys = low_back(low(qkv_mixed[1]))
    values = low_back(low(qkv_mixed[2] + b_qv[1]))
    positions = jnp.arange(length, dtype=jnp.int32)
    allowed = (segments[:, None] == segments[None, :]) & (keep_row[None, :] == 1) | (positions[:, None] == positions[None, :])

    def heads_first(tensor):
        return tensor.reshape(length, HEADS, HEAD).transpose(1, 0, 2)
    attended = lax.map(jax.checkpoint(partial(attend_head, allowed=allowed)), (heads_first(queries), heads_first(keys), heads_first(values)))
    attended = low_back(low(attended.transpose(1, 0, 2).reshape(length, D)))
    projected = low_back(jnp.dot(attended, w_attn, precision=highest))
    first_norm = layer_norm(tokens_f + projected + b_attn, ln1_gain, ln1_bias)
    first_low = low(first_norm).reshape(length, GROUPS, D // GROUPS)
    hidden = low_back(jnp.einsum('lgc,gcf->lgf', first_low, w_inter, precision=highest)) + b_inter.reshape(GROUPS, FF // GROUPS)
    activated = low(jax.nn.gelu(hidden, approximate=False))
    outward = low_back(jnp.einsum('lgf,gfd->lgd', activated, w_output, precision=highest)).reshape(length, D) + b_output
    return layer_norm(first_norm + outward, ln2_gain, ln2_bias)

def reference(tokens, w_qkv, b_qv, w_attn, b_attn, ln1_gain, ln1_bias, w_inter, b_inter, w_output, b_output, ln2_gain, ln2_bias, segment_ids, keep_mask, cotangent):
    params = tuple((weight.astype(jnp.float32) for weight in (w_qkv, b_qv, w_attn, b_attn, ln1_gain, ln1_bias, w_inter, b_inter, w_output, b_output, ln2_gain, ln2_bias)))

    def one_sequence(totals, operands):
        sequence, segments, keep_row, seed_grad = operands

        def forward(tokens_f, *weights):
            return block_forward(tokens_f, *weights, segments, keep_row)
        result, pullback = jax.vjp(forward, sequence.astype(jnp.float32), *params)
        gradients = pullback(seed_grad.astype(jnp.float32))
        totals = tuple((running + gradient for running, gradient in zip(totals, gradients[1:])))
        return (totals, (result.astype(jnp.bfloat16), gradients[0]))
    zeros_init = tuple((jnp.zeros_like(weight) for weight in params))
    totals, (outputs, token_grads) = lax.scan(one_sequence, zeros_init, (tokens, segment_ids, keep_mask, cotangent))
    return (outputs, token_grads, totals[0], totals[1], totals[2], totals[3], totals[4], totals[5], totals[6], totals[7], totals[8], totals[9], totals[10], totals[11])
```

```python
from functools import partial
import math

import jax
import jax.numpy as jnp
from jax import lax
from jax.experimental import pallas as pl
from jax.experimental.pallas import tpu as pltpu
from jax.sharding import PartitionSpec as P

HEADS = 12
HEAD = 64
GROUPS = 4


epsilon = 1e-05
masked_score = -1e30


def layer_norm(residual, gain_vec, shift_vec):
    centre = residual - jnp.mean(residual, axis=-1, keepdims=True)
    spread = jnp.mean(centre * centre, axis=-1, keepdims=True)
    return centre * lax.rsqrt(spread + epsilon) * gain_vec + shift_vec


def heads_split(tensor, head_pairs):
    lead_dim, row_count = (tensor.shape[0], tensor.shape[1])
    shaped = tensor.reshape(lead_dim, row_count, head_pairs, 2, HEAD).transpose(0, 2, 3, 1, 4)
    return shaped.reshape(lead_dim * head_pairs, 2, row_count, HEAD)


def heads_merge(tensor, lead_dim):
    block_count, row_count = (tensor.shape[0], tensor.shape[2])
    head_pairs = block_count // lead_dim
    shaped = tensor.reshape(lead_dim, head_pairs, 2, row_count, HEAD).transpose(0, 3, 1, 2, 4)
    return shaped.reshape(lead_dim, row_count, head_pairs * 2 * HEAD)


def split_blocks(tensor, width):
    return tensor.reshape(tensor.shape[0], -1, width, tensor.shape[-1]).transpose(1, 0, 2, 3)


def merge_blocks(tensor):
    return tensor.transpose(1, 0, 2, 3).reshape(tensor.shape[1], -1, tensor.shape[-1])


def allowed_mask(seg_rows, seg_cols, keep_cols, row_offset, col_offset):
    row_count = seg_rows.shape[0]
    col_count = seg_cols.shape[0]
    row_places = row_offset + jnp.arange(row_count, dtype=jnp.int32)
    col_places = col_offset + jnp.arange(col_count, dtype=jnp.int32)
    same_doc = (seg_rows[:, None] == seg_cols[None, :]) & (keep_cols[None, :] == 1)
    return same_doc | (row_places[:, None] == col_places[None, :])


def masked_scores(
    query_blk, key_piece, seg_q, seg_piece, keep_piece, row_offset, col_offset, factor
):
    allowed = allowed_mask(seg_q, seg_piece, keep_piece, row_offset, col_offset)
    scores = (
        jnp.einsum("hqd,hkd->hqk", query_blk, key_piece, preferred_element_type=jnp.float32)
        * factor
    )
    return jnp.where(allowed[None], scores, masked_score)


def body(
    tokens,
    w_qkv,
    b_qv,
    w_attn,
    b_attn,
    ln1_gain,
    ln1_bias,
    w_inter,
    b_inter,
    w_output,
    b_output,
    ln2_gain,
    ln2_bias,
    segment_ids,
    keep_mask,
    cotangent,
):
    seq_count, tok_local, model_width = tokens.shape
    head_pairs = HEADS // 2
    factor = HEAD ** (-0.5)
    length = tok_local * lax.axis_size("shard")
    block_cols = math.gcd(length, 1024)
    offset = lax.axis_index("shard") * tok_local
    flat_rows = seq_count * tok_local
    seg_own = lax.dynamic_slice_in_dim(segment_ids, offset, tok_local, 1)
    rep_own = jnp.repeat(seg_own, head_pairs, axis=0)
    rep_all = jnp.repeat(segment_ids, head_pairs, axis=0)
    rep_keep = jnp.repeat(keep_mask, head_pairs, axis=0)
    block_starts = jnp.arange(length // block_cols, dtype=jnp.int32) * block_cols
    qkv_full, bias_qv, dense_w, dense_b, gain_one, shift_one = (
        lax.all_gather(w_qkv, "shard", axis=2, tiled=True),
        lax.all_gather(b_qv, "shard", axis=1, tiled=True),
        lax.all_gather(w_attn, "shard", axis=0, tiled=True),
        lax.all_gather(b_attn, "shard", axis=0, tiled=True),
        lax.all_gather(ln1_gain, "shard", axis=0, tiled=True),
        lax.all_gather(ln1_bias, "shard", axis=0, tiled=True),
    )
    grouped = tokens.reshape(flat_rows, GROUPS, model_width // GROUPS)
    qkv_mixed = jnp.einsum(
        "rgc,kgcd->krgd", grouped, qkv_full, preferred_element_type=jnp.float32
    ).reshape(3, seq_count, tok_local, model_width)
    queries = (qkv_mixed[0] + bias_qv[0].astype(jnp.float32)).astype(jnp.bfloat16)
    keys_own = qkv_mixed[1].astype(jnp.bfloat16)
    values_own = (qkv_mixed[2] + bias_qv[1].astype(jnp.float32)).astype(jnp.bfloat16)
    keys_all, values_all = (
        lax.all_gather(keys_own, "shard", axis=1, tiled=True),
        lax.all_gather(values_own, "shard", axis=1, tiled=True),
    )
    queries_h = heads_split(queries, head_pairs)
    keys_h = heads_split(keys_all, head_pairs)
    values_h = heads_split(values_all, head_pairs)

    def forward_block(operands):
        query_blk, key_blk, value_blk, seg_q, seg_k, keep_k = operands
        keys_b = split_blocks(key_blk, block_cols)
        values_b = split_blocks(value_blk, block_cols)
        segs_b = seg_k.reshape(-1, block_cols)
        keeps_b = keep_k.reshape(-1, block_cols)
        row_shape = query_blk.shape[:2]

        def peak_step(carry, pieces):
            peak, total = carry
            key_piece, seg_piece, keep_piece, start = pieces
            masked = masked_scores(
                query_blk, key_piece, seg_q, seg_piece, keep_piece, offset, start, factor
            )
            new_peak = jnp.maximum(peak, jnp.max(masked, axis=-1))
            total = total * jnp.exp(peak - new_peak) + jnp.sum(
                jnp.exp(masked - new_peak[..., None]), axis=-1
            )
            return ((new_peak, total), None)

        (peak, total), _ = lax.scan(
            peak_step,
            (jnp.full(row_shape, masked_score, jnp.float32), jnp.zeros(row_shape, jnp.float32)),
            (keys_b, segs_b, keeps_b, block_starts),
        )
        logsum = peak + jnp.log(total)

        def value_step(acc, pieces):
            key_piece, value_piece, seg_piece, keep_piece, start = pieces
            masked = masked_scores(
                query_blk, key_piece, seg_q, seg_piece, keep_piece, offset, start, factor
            )
            prob_low = jnp.exp(masked - logsum[..., None]).astype(jnp.bfloat16)
            return (
                acc
                + jnp.einsum(
                    "hqk,hkd->hqd", prob_low, value_piece, preferred_element_type=jnp.float32
                ),
                None,
            )

        attended_blk, _ = lax.scan(
            value_step,
            jnp.zeros(query_blk.shape, jnp.float32),
            (keys_b, values_b, segs_b, keeps_b, block_starts),
        )
        return (attended_blk, logsum)

    attended_h, logsums = lax.map(
        forward_block, (queries_h, keys_h, values_h, rep_own, rep_all, rep_keep)
    )
    attended = (
        heads_merge(attended_h, seq_count).astype(jnp.bfloat16).reshape(flat_rows, model_width)
    )
    projected = jnp.dot(attended, dense_w, preferred_element_type=jnp.float32)
    resid_one = (
        tokens.reshape(flat_rows, model_width).astype(jnp.float32)
        + projected
        + dense_b.astype(jnp.float32)
    )
    first_norm, norm_one_pull = jax.vjp(
        layer_norm, resid_one, gain_one.astype(jnp.float32), shift_one.astype(jnp.float32)
    )
    first_low = first_norm.astype(jnp.bfloat16).reshape(flat_rows, GROUPS, model_width // GROUPS)
    inter_w, inter_b, out_w, out_b, gain_two, shift_two = (
        lax.all_gather(w_inter, "shard", axis=1, tiled=True),
        lax.all_gather(b_inter, "shard", axis=0, tiled=True),
        lax.all_gather(w_output, "shard", axis=1, tiled=True),
        lax.all_gather(b_output, "shard", axis=0, tiled=True),
        lax.all_gather(ln2_gain, "shard", axis=0, tiled=True),
        lax.all_gather(ln2_bias, "shard", axis=0, tiled=True),
    )
    hidden = jnp.einsum(
        "rgc,gcf->rgf", first_low, inter_w, preferred_element_type=jnp.float32
    ) + inter_b.astype(jnp.float32).reshape(GROUPS, -1)
    activated, gelu_pull = jax.vjp(partial(jax.nn.gelu, approximate=False), hidden)
    activated_low = activated.astype(jnp.bfloat16)
    outward = jnp.einsum(
        "rgf,gfd->rgd", activated_low, out_w, preferred_element_type=jnp.float32
    ).reshape(flat_rows, model_width) + out_b.astype(jnp.float32)
    normed, norm_two_pull = jax.vjp(
        layer_norm,
        first_norm + outward,
        gain_two.astype(jnp.float32),
        shift_two.astype(jnp.float32),
    )
    output = normed.astype(jnp.bfloat16).reshape(seq_count, tok_local, model_width)
    grad_out = cotangent.reshape(flat_rows, model_width).astype(jnp.float32)
    d_resid_two, d_gain_two, d_shift_two = norm_two_pull(grad_out)
    d_out_b = jnp.sum(d_resid_two, axis=0)
    d_out_low = d_resid_two.astype(jnp.bfloat16).reshape(flat_rows, GROUPS, -1)
    d_out_w = jnp.einsum(
        "rgf,rgd->gfd", activated_low, d_out_low, preferred_element_type=jnp.float32
    )
    d_activated = jnp.einsum("rgd,gfd->rgf", d_out_low, out_w, preferred_element_type=jnp.float32)
    (d_hidden,) = gelu_pull(d_activated)
    d_inter_b = jnp.sum(d_hidden, axis=0).reshape(-1)
    d_hidden_low = d_hidden.astype(jnp.bfloat16)
    d_inter_w = jnp.einsum(
        "rgc,rgf->gcf", first_low, d_hidden_low, preferred_element_type=jnp.float32
    )
    d_first = d_resid_two + jnp.einsum(
        "rgf,gcf->rgc", d_hidden_low, inter_w, preferred_element_type=jnp.float32
    ).reshape(flat_rows, model_width)
    d_resid_one, d_gain_one, d_shift_one = norm_one_pull(d_first)
    d_dense_b = jnp.sum(d_resid_one, axis=0)
    d_proj_low = d_resid_one.astype(jnp.bfloat16)
    d_dense_w = jnp.einsum("rc,rd->cd", attended, d_proj_low, preferred_element_type=jnp.float32)
    d_attended = (
        jnp.einsum("rd,cd->rc", d_proj_low, dense_w, preferred_element_type=jnp.float32)
        .astype(jnp.bfloat16)
        .reshape(seq_count, tok_local, model_width)
    )
    d_attended_h = heads_split(d_attended, head_pairs)

    def query_back(operands, with_keys):
        query_blk, key_blk, value_blk, grad_blk, logsum_blk, seg_q, seg_k, keep_k = operands
        keys_b = split_blocks(key_blk, block_cols)
        values_b = split_blocks(value_blk, block_cols)
        segs_b = seg_k.reshape(-1, block_cols)
        keeps_b = keep_k.reshape(-1, block_cols)
        pieces_all = (keys_b, values_b, segs_b, keeps_b, block_starts)

        def inner_step(acc, pieces):
            key_piece, value_piece, seg_piece, keep_piece, start = pieces
            masked = masked_scores(
                query_blk, key_piece, seg_q, seg_piece, keep_piece, offset, start, factor
            )
            prob_full = jnp.exp(masked - logsum_blk[..., None])
            d_probs = jnp.einsum(
                "hqd,hkd->hqk", grad_blk, value_piece, preferred_element_type=jnp.float32
            )
            return (acc + jnp.sum(prob_full * d_probs, axis=-1), None)

        inner_prod, _ = lax.scan(inner_step, jnp.zeros(logsum_blk.shape, jnp.float32), pieces_all)

        def grad_step(d_query, pieces):
            key_piece, value_piece, seg_piece, keep_piece, start = pieces
            masked = masked_scores(
                query_blk, key_piece, seg_q, seg_piece, keep_piece, offset, start, factor
            )
            prob_full = jnp.exp(masked - logsum_blk[..., None])
            d_probs = jnp.einsum(
                "hqd,hkd->hqk", grad_blk, value_piece, preferred_element_type=jnp.float32
            )
            d_scores = (prob_full * (d_probs - inner_prod[..., None])).astype(jnp.bfloat16)
            d_query = (
                d_query
                + jnp.einsum(
                    "hqk,hkd->hqd", d_scores, key_piece, preferred_element_type=jnp.float32
                )
                * factor
            )
            d_key = (
                jnp.einsum("hqk,hqd->hkd", d_scores, query_blk, preferred_element_type=jnp.float32)
                * factor
            )
            d_value = jnp.einsum(
                "hqk,hqd->hkd",
                prob_full.astype(jnp.bfloat16),
                grad_blk,
                preferred_element_type=jnp.float32,
            )
            return (d_query, (d_key, d_value))

        d_query, key_terms = lax.scan(
            grad_step, jnp.zeros(query_blk.shape, jnp.float32), pieces_all
        )
        return (d_query, merge_blocks(key_terms[0]), merge_blocks(key_terms[1]))

    d_query_h, d_key_h, d_value_h = lax.map(
        partial(query_back, with_keys=True),
        (queries_h, keys_h, values_h, d_attended_h, logsums, rep_own, rep_all, rep_keep),
    )
    d_keys_part = heads_merge(d_key_h, seq_count)
    d_values_part = heads_merge(d_value_h, seq_count)
    d_keys, d_values = (
        lax.psum_scatter(d_keys_part, "shard", scatter_dimension=1, tiled=True),
        lax.psum_scatter(d_values_part, "shard", scatter_dimension=1, tiled=True),
    )
    d_queries = heads_merge(d_query_h, seq_count)
    d_stack = (
        jnp.stack([d_queries, d_keys, d_values])
        .astype(jnp.bfloat16)
        .reshape(3, flat_rows, GROUPS, model_width // GROUPS)
    )
    d_qkv_w = jnp.einsum("rgc,krgd->kgcd", grouped, d_stack, preferred_element_type=jnp.float32)
    d_bias_qv = jnp.stack(
        [
            jnp.sum(d_stack[0].astype(jnp.float32), axis=0).reshape(-1),
            jnp.sum(d_stack[2].astype(jnp.float32), axis=0).reshape(-1),
        ]
    )
    d_tokens = d_resid_one + jnp.einsum(
        "krgd,kgcd->rgc", d_stack, qkv_full, preferred_element_type=jnp.float32
    ).reshape(flat_rows, model_width)
    (
        g_qkv,
        g_bqv,
        g_dense,
        g_dense_b,
        g_gain_one,
        g_shift_one,
        g_inter,
        g_inter_b,
        g_out,
        g_out_b,
        g_gain_two,
        g_shift_two,
    ) = (
        lax.psum_scatter(d_qkv_w, "shard", scatter_dimension=2, tiled=True),
        lax.psum_scatter(d_bias_qv, "shard", scatter_dimension=1, tiled=True),
        lax.psum_scatter(d_dense_w, "shard", scatter_dimension=0, tiled=True),
        lax.psum_scatter(d_dense_b, "shard", scatter_dimension=0, tiled=True),
        lax.psum_scatter(d_gain_one, "shard", scatter_dimension=0, tiled=True),
        lax.psum_scatter(d_shift_one, "shard", scatter_dimension=0, tiled=True),
        lax.psum_scatter(d_inter_w, "shard", scatter_dimension=1, tiled=True),
        lax.psum_scatter(d_inter_b, "shard", scatter_dimension=0, tiled=True),
        lax.psum_scatter(d_out_w, "shard", scatter_dimension=1, tiled=True),
        lax.psum_scatter(d_out_b, "shard", scatter_dimension=0, tiled=True),
        lax.psum_scatter(d_gain_two, "shard", scatter_dimension=0, tiled=True),
        lax.psum_scatter(d_shift_two, "shard", scatter_dimension=0, tiled=True),
    )
    summed = lax.psum(
        (
            g_qkv,
            g_bqv,
            g_dense,
            g_dense_b,
            g_gain_one,
            g_shift_one,
            g_inter,
            g_inter_b,
            g_out,
            g_out_b,
            g_gain_two,
            g_shift_two,
        ),
        "rep",
    )
    return (
        output,
        d_tokens.reshape(seq_count, tok_local, model_width),
        summed[0],
        summed[1],
        summed[2],
        summed[3],
        summed[4],
        summed[5],
        summed[6],
        summed[7],
        summed[8],
        summed[9],
        summed[10],
        summed[11],
    )


BF = jnp.bfloat16
F32 = jnp.float32
I32 = jnp.int32
VEC_ROWS = 16
ROW_SPLIT = 4


def mxu(a, b, dims):
    return lax.dot_general(a, b, (dims, ((), ())), preferred_element_type=F32)


def nn(a, b):
    return mxu(a, b, ((1,), (0,)))


def nt(a, b):
    return mxu(a, b, ((1,), (1,)))


def tn(a, b):
    return mxu(a, b, ((0,), (0,)))


def vmem(n):
    return [pl.BlockSpec(memory_space=pltpu.VMEM)] * n


def smem():
    return pl.BlockSpec(memory_space=pltpu.SMEM)


def call(kernel, outs, scratch=(), limit=None, name=None, cost=None):
    def go(place, *args):
        return pl.pallas_call(
            kernel,
            out_shape=outs,
            in_specs=[smem()] + vmem(len(args)),
            out_specs=tuple(vmem(len(outs))),
            scratch_shapes=list(scratch),
            compiler_params=pltpu.CompilerParams(vmem_limit_bytes=limit or (40 << 20)),
            name=name,
            cost_estimate=cost,
        )(place, *args)

    return go


def aligned(index, size):
    return pl.ds(pl.multiple_of(index * size, size), size)


def packet_kernel(place, tokens, w_qkv, vectors, b_inter, *refs):
    packets, turned = refs[:4], refs[4]
    s = place[0]
    rows, width = tokens.shape
    part = width // 4
    turned[...] = tokens[...].T
    own = w_qkv.shape[2]
    for d in range(4):
        to = s ^ d
        packets[d][0:part, :] = turned[aligned(to, part), :]
        for t in range(3):
            packets[d][part + t * own : part + (t + 1) * own, 0:part] = w_qkv[t, to]
        packets[d][part + 3 * own :, :] = jnp.zeros((packets[d].shape[0] - part - 3 * own, rows), BF)
    base = part + 3 * own
    count = vectors.shape[0]
    for shard in range(4):

        @pl.when(s == shard)
        def _():
            spread = jnp.concatenate(
                [jnp.zeros((count, part * shard), BF)] * (shard > 0)
                + [vectors[...]]
                + [jnp.zeros((count, part * (3 - shard)), BF)] * (shard < 3),
                axis=1,
            )
            lines = jnp.concatenate(
                [jnp.zeros((1, width), BF)] * shard + [b_inter[...]] + [jnp.zeros((1, width), BF)] * (3 - shard),
                axis=0,
            )
            for piece in range(width // rows):
                at = slice(rows * piece, rows * (piece + 1))
                for d in range(4):
                    top = base + VEC_ROWS * piece
                    packets[d][top : top + count, :] = spread[:, at]
                    packets[d][top + 8 : top + 12, :] = lines[:, at]


def attention_kernel(place, p0, p1, p2, p3, bias_qv, segments, keep, *refs):
    (o0, o1, o2, o3, weights, shares, inverse, q_all, k_all, v_all, w_all, k_rows, mask) = refs
    packets, outs = (p0, p1, p2, p3), (o0, o1, o2, o3)
    s = place[0]
    head = pl.program_id(0)
    block = o0.shape[1]
    part = o0.shape[0]
    own = part // 4
    length = 4 * block

    @pl.when(head == 0)
    def _():
        for d in range(4):
            for t in range(3):
                w_all[t, aligned(s ^ d, own), :] = packets[d][part + t * own : part + (t + 1) * own, 0:part]
        for d in range(4):
            cols = slice(block * d, block * (d + 1))
            x = packets[d][0:part, :]
            q = tn(w_all[0], x) + bias_qv[:, 0:1].astype(F32)
            q_all[:, cols] = (q.astype(BF).astype(F32) * HEAD ** (-0.5)).astype(BF)
            k_all[:, cols] = tn(w_all[1], x).astype(BF)
            v_all[:, cols] = (tn(w_all[2], x) + bias_qv[:, 1:2].astype(F32)).astype(BF)
        for h in range(part // HEAD):
            k_rows[h] = k_all[HEAD * h : HEAD * (h + 1), :].T
        seg_row = jnp.concatenate([segments[:, aligned(s ^ d, block)] for d in range(4)], axis=1)
        for d in range(4):
            code = jnp.where(keep[:, aligned(s ^ d, block)] == 1, segments[:, aligned(s ^ d, block)], -1)
            column = jnp.broadcast_to(code.astype(F32), (128, block)).T
            for c in range(4):
                want = jnp.broadcast_to(seg_row[:, block * c : block * (c + 1)].astype(F32), (block, block))
                same = jnp.concatenate([column] * (block // 128), axis=1) == want
                if c == d:
                    same = same | (
                        lax.broadcasted_iota(I32, (block, block), 0) == lax.broadcasted_iota(I32, (block, block), 1)
                    )
                mask[block * d : block * (d + 1), block * c : block * (c + 1)] = jnp.where(same, 0.0, masked_score)

    rows = aligned(head, HEAD)
    for c in range(4):
        cols = slice(block * c, block * (c + 1))
        scores = nn(k_rows[head], q_all[rows, cols]) + mask[:, cols]
        peak = jnp.max(scores, axis=0, keepdims=True)
        terms = jnp.exp(scores - peak)
        inv = 1.0 / jnp.sum(terms, axis=0, keepdims=True)
        low = terms.astype(BF)
        shares[0, :, cols] = low
        inverse[head, :, cols] = inv
        outs[c][rows, :] = (nn(v_all[rows, :], low) * inv).astype(BF)

    @pl.when(head == 0)
    def _():
        weights[...] = w_all[...]


def attention_forward(place, packets, bias_qv, segments, keep):
    part = bias_qv.shape[0]
    block = packets[0].shape[1]
    length = 4 * block
    heads = part // HEAD
    whole = lambda shape: pl.BlockSpec(shape, lambda h: (0,) * len(shape))
    sd = jax.ShapeDtypeStruct
    outs = [sd((part, block), BF)] * 4 + [
        sd((3, part, part), BF),
        sd((heads, length, length), BF),
        sd((heads, 1, length), F32),
        sd((part, length), BF),
        sd((part, length), BF),
        sd((part, length), BF),
    ]
    out_specs = [whole(o.shape) for o in outs]
    out_specs[5] = pl.BlockSpec((1, length, length), lambda h: (h, 0, 0))
    args = (*packets, bias_qv, segments, keep)
    return pl.pallas_call(
        attention_kernel,
        grid=(heads,),
        out_shape=outs,
        in_specs=[smem()] + [whole(a.shape) for a in args],
        out_specs=out_specs,
        scratch_shapes=[
            pltpu.VMEM((3, part, part), BF),
            pltpu.VMEM((heads, length, HEAD), BF),
            pltpu.VMEM((length, length), F32),
        ],
        compiler_params=pltpu.CompilerParams(vmem_limit_bytes=48 << 20),
        name="attention_forward",
    )(place, *args)


def attention_back_kernel(place, g0, g1, g2, g3, o0, o1, o2, o3, p0, p1, p2, p3, weights, shares, inverse, q_all, k_all, v_all, *refs):
    (t0, t1, t2, t3, w0, w1, w2, w3, g_bias, d_q, d_k, d_v, marks) = refs
    grads, outs, packets = (g0, g1, g2, g3), (o0, o1, o2, o3), (p0, p1, p2, p3)
    s = place[0]
    head = pl.program_id(0)
    heads = pl.num_programs(0)
    block = g0.shape[1]
    part = g0.shape[0]
    own = part // 4
    rows = aligned(head, HEAD)
    v_rows = v_all[rows, :].T
    lows = []
    for c in range(4):
        cols = slice(block * c, block * (c + 1))
        grad = grads[c][rows, :].astype(F32) * inverse[head, :, cols]
        low = grad.astype(BF)
        lows.append(low)
        inner = jnp.sum(grad * outs[c][rows, :].astype(F32), axis=0, keepdims=True)
        d_share = nn(v_rows, low)
        marks[:, cols] = (shares[0, :, cols].astype(F32) * (d_share - inner)).astype(BF)
        d_q[rows, cols] = (nn(k_all[rows, :], marks[:, cols]) * HEAD ** (-0.5)).astype(BF)
    d_k[rows, :] = nt(q_all[rows, :], marks[...]).astype(BF)
    d_v[rows, :] = nt(jnp.concatenate(lows, axis=1), shares[0]).astype(BF)

    @pl.when(head == heads - 1)
    def _():
        x = jnp.concatenate([p[0:part, :] for p in packets], axis=1)
        outgoing = (t0, t1, t2, t3)
        for c in range(4):
            cols = slice(block * c, block * (c + 1))
            outgoing[c][...] = (
                nn(weights[0], d_q[:, cols]) + nn(weights[1], d_k[:, cols]) + nn(weights[2], d_v[:, cols])
            ).astype(BF)
        totals = (w0, w1, w2, w3)
        for t, d in enumerate((d_q, d_k, d_v)):
            g = nt(x, d[...])
            marks[t * part : (t + 1) * part, 0:part] = g.astype(BF)
        for d in range(4):
            for t in range(3):
                start = pl.multiple_of(t * part + (s ^ d) * own, own)
                totals[d][t * own : (t + 1) * own, :] = marks[pl.ds(start, own), 0:part]
        ones = jnp.ones((8, 4 * block), BF)
        g_bias[0:8, :] = nt(ones, d_q[...])
        g_bias[8:16, :] = nt(ones, d_v[...])


def attention_backward(place, grads, outs, packets, weights, shares, inverse, q_all, k_all, v_all):
    part, block = grads[0].shape
    length = 4 * block
    heads = part // HEAD
    own = part // 4
    whole = lambda shape: pl.BlockSpec(shape, lambda h: (0,) * len(shape))
    sd = jax.ShapeDtypeStruct
    args = (*grads, *outs, *packets, weights, shares, inverse, q_all, k_all, v_all)
    in_specs = [whole(a.shape) for a in args]
    in_specs[13] = pl.BlockSpec((1, length, length), lambda h: (h, 0, 0))
    results = [sd((part, block), BF)] * 4 + [sd((3 * own, part), BF)] * 4 + [sd((16, part), F32)]
    return pl.pallas_call(
        attention_back_kernel,
        grid=(heads,),
        out_shape=results,
        in_specs=[smem()] + in_specs,
        out_specs=[whole(o.shape) for o in results],
        scratch_shapes=[
            pltpu.VMEM((part, length), BF),
            pltpu.VMEM((part, length), BF),
            pltpu.VMEM((part, length), BF),
            pltpu.VMEM((length, length), BF),
        ],
        compiler_params=pltpu.CompilerParams(vmem_limit_bytes=48 << 20),
        name="attention_backward",
    )(place, *args)


def eighth_kernel(place, w_attn, w_inter, w_output, out, dense):
    chip, core = place[1], place[2]
    part = w_attn.shape[0]
    width = w_attn.shape[1]
    rows, cols = part // ROW_SPLIT, width // 2
    for g in range(4):
        dense[:, part * g : part * (g + 1)] = w_output[g]
    take = aligned(chip, rows)
    for half in range(2):

        @pl.when(core == half)
        def _():
            lanes = slice(cols * half, cols * (half + 1))
            out[0:rows, :] = w_attn[take, lanes]
            out[rows : 2 * rows, :] = w_inter[chip, :, lanes]
            out[2 * rows : 3 * rows, :] = dense[take, lanes]


def rows_mean(v):
    return jnp.mean(v, axis=1, keepdims=True)


def middle_kernel(place, a0, a1, a2, a3, p0, p1, p2, p3, tokens, cotangent, *refs):
    weights, refs = refs[:8], refs[8:]
    (output, d_resid_one_out, b0, b1, b2, b3, keep_out, send_out, w_attn, w_inter, w_out, att, act, slope, grads, back) = refs
    s, chip, core = place[0], place[1], place[2]
    rows, width = tokens.shape
    part = width // 4
    piece_rows = part // ROW_SPLIT
    half = width // 2

    def place_weights(c, lanes):
        for q in range(4):
            for d in range(4):
                ref, top = weights[c * 4 + q], 3 * piece_rows * d
                start = pl.multiple_of((s ^ d) * part + (chip ^ q) * piece_rows, piece_rows)
                w_attn[pl.ds(start, piece_rows), lanes] = ref[top : top + piece_rows, :]
                w_inter[chip ^ q, aligned(s ^ d, piece_rows), lanes] = ref[top + piece_rows : top + 2 * piece_rows, :]
                w_out[pl.ds(start, piece_rows), lanes] = ref[top + 2 * piece_rows : top + 3 * piece_rows, :]

    for lane_half in range(2):
        lanes = slice(half * lane_half, half * (lane_half + 1))

        @pl.when(core == lane_half)
        def _():
            place_weights(0, lanes)

        @pl.when(core != lane_half)
        def _():
            place_weights(1, lanes)

    packets = (p0, p1, p2, p3)
    base = part + 3 * piece_rows
    vec = jnp.concatenate(
        [
            sum(p[base + VEC_ROWS * i : base + VEC_ROWS * (i + 1), :].astype(F32) for p in packets)
            for i in range(width // rows)
        ],
        axis=1,
    )
    b_attn, gain_one, shift_one, b_output, gain_two, shift_two = (vec[i : i + 1, :] for i in range(6))

    for d, ref in enumerate((a0, a1, a2, a3)):
        att[aligned(s ^ d, part), :] = ref[...]
    resid = tokens[...].astype(F32) + tn(att[...], w_attn[...]) + b_attn
    centre = resid - rows_mean(resid)
    inv_one = lax.rsqrt(rows_mean(centre * centre) + epsilon)
    norm_one = centre * inv_one
    first = norm_one * gain_one + shift_one
    first_low = first.astype(BF)

    outward = []
    for g in range(4):
        x = first_low[:, part * g : part * (g + 1)]
        hidden = nn(x, w_inter[g]) + vec[8 + g : 9 + g, :]
        phi = 0.5 + 0.5 * lax.erf(hidden * (0.5**0.5))
        low = (hidden * phi).astype(BF)
        act[g] = low
        slope[g] = phi + hidden * (jnp.exp(-0.5 * hidden * hidden) * ((2.0 * math.pi) ** -0.5))
        outward.append(nn(low, w_out[:, part * g : part * (g + 1)]))
    resid = first + jnp.concatenate(outward, axis=1) + b_output
    centre = resid - rows_mean(resid)
    inv_two = lax.rsqrt(rows_mean(centre * centre) + epsilon)
    norm_two = centre * inv_two
    output[...] = (norm_two * gain_two + shift_two).astype(BF)

    cot = cotangent[...].astype(F32)
    total = lambda v: jnp.sum(v, axis=0, keepdims=True)
    grad_gain_two, grad_shift_two = total(cot * norm_two), total(cot)
    e_two = cot * gain_two
    d_resid = inv_two * (e_two - rows_mean(e_two) - norm_two * rows_mean(e_two * norm_two))
    grad_b_output = total(d_resid)
    d_low = d_resid.astype(BF)
    d_first, grad_b_inter = [], []
    for g in range(4):
        lanes = slice(part * g, part * (g + 1))
        x = first_low[:, lanes]
        dl = d_low[:, lanes]
        grads[2 * width : 3 * width, lanes] = tn(act[g], dl).astype(BF)
        d_hidden = nt(dl, w_out[:, lanes]) * slope[g]
        grad_b_inter.append(total(d_hidden))
        dh = d_hidden.astype(BF)
        grads[width + part * g : width + part * (g + 1), :] = tn(x, dh).astype(BF)
        d_first.append(nt(dh, w_inter[g]))
    d_first = d_resid + jnp.concatenate(d_first, axis=1)
    grad_gain_one, grad_shift_one = total(d_first * norm_one), total(d_first)
    e_one = d_first * gain_one
    d_one = inv_one * (e_one - rows_mean(e_one) - norm_one * rows_mean(e_one * norm_one))
    d_resid_one_out[...] = d_one
    grad_b_attn = total(d_one)
    d_proj = d_one.astype(BF)
    grads[0:width, :] = nn(att[...], d_proj).astype(BF)
    back[...] = nt(w_attn[...], d_proj).astype(BF)
    for d, ref in enumerate((b0, b1, b2, b3)):
        ref[...] = back[aligned(s ^ d, part), :]

    vec_grads = jnp.concatenate(
        [grad_b_attn, grad_gain_one, grad_shift_one, grad_b_output, grad_gain_two, grad_shift_two]
        + [jnp.zeros((2, width), F32)]
        + grad_b_inter
        + [jnp.zeros((4, width), F32)],
        axis=0,
    )
    high = vec_grads.astype(BF)
    rest = (vec_grads - high.astype(F32)).astype(BF)
    for ref, flip in ((keep_out, 0), (send_out, 1)):
        for lane_half in range(2):

            @pl.when((core ^ flip) == lane_half)
            def _():
                lanes = slice(half * lane_half, half * (lane_half + 1))
                for q in range(4):
                    for d in range(4):
                        top = (q * 4 + d) * 3 * piece_rows
                        start = pl.multiple_of((s ^ d) * part + (chip ^ q) * piece_rows, piece_rows)
                        inter = pl.multiple_of(width + (chip ^ q) * part + (s ^ d) * piece_rows, piece_rows)
                        ref[top : top + piece_rows, :] = grads[pl.ds(start, piece_rows), lanes]
                        ref[top + piece_rows : top + 2 * piece_rows, :] = grads[pl.ds(inter, piece_rows), lanes]
                        ref[top + 2 * piece_rows : top + 3 * piece_rows, :] = grads[
                            pl.ds(2 * width + start, piece_rows), lanes
                        ]

        top = 16 * 3 * piece_rows
        ref[top : top + 16, :] = high[:, 0:half]
        ref[top + 16 : top + 32, :] = high[:, half:width]
        ref[top + 32 : top + 48, :] = rest[:, 0:half]
        ref[top + 48 : top + 64, :] = rest[:, half:width]


def join_kernel(place, *refs):
    pieces, out = refs[:-1], refs[-1]
    for i, piece in enumerate(pieces):
        out[piece.shape[0] * i : piece.shape[0] * (i + 1), :] = piece[...]


def split_low(v):
    high = v.astype(BF)
    return high, (v - high.astype(F32)).astype(BF)


def tree(terms):
    a, b, c, d = terms
    return (a + b) + (c + d)


def vec_of(ref, top):
    return ref[top : top + 32, :].astype(F32) + ref[top + 32 : top + 64, :].astype(F32)


def core_sum_kernel(place, mine, theirs, *outs):
    piece = (mine.shape[0] - 64) // 4
    high, rest = split_low(vec_of(mine, 4 * piece) + vec_of(theirs, 4 * piece))
    for q, out in enumerate(outs):
        rows = slice(piece * q, piece * (q + 1))
        out[0:piece, :] = (mine[rows, :].astype(F32) + theirs[rows, :].astype(F32)).astype(BF)
        out[piece : piece + 32, :] = high
        out[piece + 32 : piece + 64, :] = rest


def chip_sum_kernel(place, m0, m1, m2, m3, *outs):
    whole = m0.shape[0] - 64
    piece = whole // 4
    parts = (m0, m1, m2, m3)
    high, rest = split_low(tree(vec_of(m, whole) for m in parts))
    for d, out in enumerate(outs):
        rows = slice(piece * d, piece * (d + 1))
        out[0:piece, :] = tree(m[rows, :].astype(F32) for m in parts).astype(BF)
        out[piece : piece + 32, :] = high
        out[piece + 32 : piece + 64, :] = rest


def shard_sum_kernel(place, m0, m1, m2, m3, out, vec):
    piece = m0.shape[0] - 64
    parts = (m0, m1, m2, m3)
    vec[...] = tree(vec_of(m, piece) for m in parts)
    out[...] = tree(m[0:piece, :].astype(F32) for m in parts).astype(BF)


def finish_kernel(place, vec, n0, n1, n2, n3, f0, f1, f2, f3, g_attn, g_inter, g_out, g_vec, g_lines, dense):
    s, chip, core = place[0], place[1], place[2]
    part, width = g_attn.shape
    rows = part // ROW_SPLIT
    half = width // 2

    def place_half(pieces, lanes):
        for q, ref in enumerate(pieces):
            at = aligned(chip ^ q, rows)
            g_attn[at, lanes] = ref[0:rows, :].astype(F32)
            g_inter[chip ^ q, :, lanes] = ref[rows : 2 * rows, :].astype(F32)
            dense[at, lanes] = ref[2 * rows : 3 * rows, :].astype(F32)

    for lane_half in range(2):
        lanes = slice(half * lane_half, half * (lane_half + 1))

        @pl.when(core == lane_half)
        def _():
            place_half((n0, n1, n2, n3), lanes)

        @pl.when(core != lane_half)
        def _():
            place_half((f0, f1, f2, f3), lanes)

    for g in range(4):
        g_out[g] = dense[:, part * g : part * (g + 1)]
    full = jnp.concatenate([vec[0:16, :], vec[16:32, :]], axis=1)
    for shard in range(4):

        @pl.when(s == shard)
        def _():
            g_vec[...] = full[0:8, part * shard : part * (shard + 1)]
            g_lines[...] = full[8 + shard : 9 + shard, :]


def qkv_core_kernel(place, w0, w1, w2, w3, v0, v1, v2, v3, b_mine, b_theirs, out):
    core = place[2]
    rows = w0.shape[0]
    mine, theirs = (w0, w1, w2, w3), (v0, v1, v2, v3)
    for c in range(2):

        @pl.when(core == c)
        def _():
            for i in range(2):
                total = mine[2 * c + i][...].astype(F32) + theirs[2 * c + i][...].astype(F32)
                out[rows * i : rows * (i + 1), :] = total.astype(BF)

    high, rest = split_low(b_mine[...] + b_theirs[...])
    out[2 * rows : 2 * rows + 16, :] = high
    out[2 * rows + 16 : 2 * rows + 32, :] = rest


def qkv_chip_kernel(place, m0, m1, m2, m3, out, bias):
    rows = m0.shape[0] - 32
    parts = (m0, m1, m2, m3)
    out[...] = tree(m[0:rows, :].astype(F32) for m in parts).astype(BF)
    bias[...] = tree(
        m[rows : rows + 16, :].astype(F32) + m[rows + 16 : rows + 32, :].astype(F32) for m in parts
    )


def qkv_finish_kernel(place, near, far, bias, g_w, g_b):
    s, core = place[0], place[2]
    own = g_w.shape[2]
    for c in range(2):

        @pl.when(core == c)
        def _():
            for i in range(2):
                for t in range(3):
                    rows = slice((3 * i + t) * own, (3 * i + t + 1) * own)
                    g_w[t, s ^ (2 * c + i)] = near[rows, :].astype(F32)
                    g_w[t, s ^ (2 - 2 * c + i)] = far[rows, :].astype(F32)

    g_b[0:1, :] = bias[0:1, :]
    g_b[1:2, :] = bias[8:9, :]


def tokens_kernel(place, d_resid, t0, t1, t2, t3, out, gathered):
    s = place[0]
    part = t0.shape[0]
    for d, ref in enumerate((t0, t1, t2, t3)):
        gathered[aligned(s ^ d, part), :] = ref[...]
    out[...] = d_resid[...] + gathered[...].astype(F32).T


def swap(x, axis, flip):
    return lax.ppermute(x, axis, [(i, i ^ flip) for i in range(lax.axis_size(axis))])


CHIPS = (2, 4, 6)


def fast_body(
    tokens, w_qkv, b_qv, w_attn, b_attn, ln1_gain, ln1_bias, w_inter, b_inter, w_output, b_output, ln2_gain, ln2_bias,
    segment_ids, keep_mask, cotangent,
):
    sd = jax.ShapeDtypeStruct
    rows, width = tokens.shape[1:]
    part, half = width // 4, width // 2
    own = part // 4
    shard, rep = lax.axis_index("shard"), lax.axis_index("rep")
    place = jnp.stack([shard, rep // 2, rep % 2]).astype(I32)
    x = tokens.reshape(rows, width)

    vectors = jnp.stack([b_attn, ln1_gain, ln1_bias, b_output, ln2_gain, ln2_bias, b_attn, b_attn])
    height = part + 3 * own + VEC_ROWS * (width // rows)
    *packets, _ = call(packet_kernel, [sd((height, rows), BF)] * 4 + [sd((width, rows), BF)], name="packets")(
        place, x, w_qkv, vectors, b_inter.reshape(1, -1)
    )
    packets = [packets[0]] + [swap(packets[d], "shard", d) for d in (1, 2, 3)]

    (eighth,) = call(eighth_kernel, [sd((3 * own, half), BF)], [pltpu.VMEM((part, width), BF)], name="eighth")(
        place, w_attn, w_inter, w_output
    )
    eighths = [eighth] + [swap(eighth, "shard", d) for d in (1, 2, 3)]
    (joined,) = call(join_kernel, [sd((12 * own, half), BF)], name="join")(place, *eighths)
    near = [joined] + [swap(joined, "rep", c) for c in CHIPS]
    weights = near + [swap(n, "rep", 1) for n in near]

    *outs, w_all, shares, inverse, q_all, k_all, v_all = attention_forward(
        place, packets, b_qv.T, segment_ids, keep_mask
    )
    attended = [outs[0]] + [swap(outs[d], "shard", d) for d in (1, 2, 3)]

    total = 48 * own + 64
    output, d_resid_one, *back, keep_part, send_part = call(
        middle_kernel,
        [sd((rows, width), BF), sd((rows, width), F32)] + [sd((part, rows), BF)] * 4 + [sd((total, half), BF)] * 2,
        [
            pltpu.VMEM((width, width), BF),
            pltpu.VMEM((4, part, width), BF),
            pltpu.VMEM((width, width), BF),
            pltpu.VMEM((width, rows), BF),
            pltpu.VMEM((4, rows, width), BF),
            pltpu.VMEM((4, rows, width), F32),
            pltpu.VMEM((3 * width, width), BF),
            pltpu.VMEM((width, rows), BF),
        ],
        limit=56 << 20,
        name="middle",
    )(place, *attended, *packets, x, cotangent.reshape(rows, width), *weights)
    d_attended = [back[0]] + [swap(back[d], "shard", d) for d in (1, 2, 3)]

    by_chip = call(core_sum_kernel, [sd((12 * own + 64, half), BF)] * 4, name="core_sum")(
        place, keep_part, swap(send_part, "rep", 1)
    )
    by_shard = call(chip_sum_kernel, [sd((3 * own + 64, half), BF)] * 4, name="chip_sum")(
        place, by_chip[0], *(swap(by_chip[q], "rep", c) for q, c in ((1, 2), (2, 4), (3, 6)))
    )
    summed, vec = call(shard_sum_kernel, [sd((3 * own, half), BF), sd((32, half), F32)], name="shard_sum")(
        place, by_shard[0], *(swap(by_shard[d], "shard", d) for d in (1, 2, 3))
    )
    near = [summed] + [swap(summed, "rep", c) for c in CHIPS]
    g_attn, g_inter, g_out, g_vec, g_lines = call(
        finish_kernel,
        [sd((part, width), F32), sd((4, own, width), F32), sd((4, part, part), F32), sd((8, part), F32), sd((1, width), F32)],
        [pltpu.VMEM((part, width), F32)],
        name="finish",
    )(place, vec, *near, *(swap(n, "rep", 1) for n in near))

    results = attention_backward(
        place, d_attended, outs, packets, w_all, shares, inverse, q_all, k_all, v_all
    )
    d_parts, w_parts, g_bias = results[:4], results[4:8], results[8]
    d_parts = [d_parts[0]] + [swap(d_parts[d], "shard", d) for d in (1, 2, 3)]
    w_parts = [w_parts[0]] + [swap(w_parts[d], "shard", d) for d in (1, 2, 3)]
    (d_tokens,) = call(tokens_kernel, [sd((rows, width), F32)], [pltpu.VMEM((width, rows), BF)], name="d_tokens")(
        place, d_resid_one, *d_parts
    )
    (mine,) = call(qkv_core_kernel, [sd((6 * own + 32, part), BF)], name="qkv_core")(
        place, *w_parts, *(swap(w, "rep", 1) for w in w_parts), g_bias, swap(g_bias, "rep", 1)
    )
    half_sum, bias_sum = call(qkv_chip_kernel, [sd((6 * own, part), BF), sd((16, part), F32)], name="qkv_chip")(
        place, mine, *(swap(mine, "rep", c) for c in CHIPS)
    )
    g_qkv, g_bqv = call(qkv_finish_kernel, [sd((3, 4, own, part), F32), sd((2, part), F32)], name="qkv_finish")(
        place, half_sum, swap(half_sum, "rep", 1), bias_sum
    )
    return (
        output[None],
        d_tokens[None],
        g_qkv,
        g_bqv,
        g_attn,
        g_vec[0],
        g_vec[1],
        g_vec[2],
        g_inter,
        g_lines[0],
        g_out,
        g_vec[3],
        g_vec[4],
        g_vec[5],
    )


def fits_fast(mesh):
    return mesh.shape["shard"] == GROUPS == 4 and mesh.shape["rep"] == 8


def solution(mesh):
    in_specs = (
        P("rep", "shard", None),
        P(None, None, "shard", None),
        P(None, "shard"),
        P("shard", None),
        P("shard"),
        P("shard"),
        P("shard"),
        P(None, "shard", None),
        P("shard"),
        P(None, "shard", None),
        P("shard"),
        P("shard"),
        P("shard"),
        P("rep", None),
        P("rep", None),
        P("rep", "shard", None),
    )
    out_specs = (
        P("rep", "shard", None),
        P("rep", "shard", None),
        P(None, None, "shard", None),
        P(None, "shard"),
        P("shard", None),
        P("shard"),
        P("shard"),
        P("shard"),
        P(None, "shard", None),
        P("shard"),
        P(None, "shard", None),
        P("shard"),
        P("shard"),
        P("shard"),
    )
    plan = fast_body if fits_fast(mesh) else body
    return jax.shard_map(plan, mesh=mesh, in_specs=in_specs, out_specs=out_specs, check_vma=False)
```
